32 devices in a mesh: scen: 2 (over y), lag: 4 (over z), elem: 4 (over x, core).
Axes of the slice: x: 2, y: 2, z: 4, core: 2. Of those that a mesh axis runs over, the one named last changes fastest.
Arguments:
- kernel: bfloat16 [16, 2048, 2048], P('lag', 'elem'), may hold values from -0.03125 to 0.03125
- past_rate: bfloat16 [16, 256, 2048], P('lag', 'scen'), parts along dimension 1, may hold values from 0 to 1
- loading: float32 [256, 2048], P('scen', 'elem'), parts along dimension 0, may hold values from -6 to 6
- initial_slip: float32 [256, 2048], P('scen', 'elem'), parts along dimension 0, may hold values from 0 to 1
- peak_strength: float32 [2048], P('elem'), may hold values from 0.5 to 2
- cohesive_flags: int32 [2048], P('elem'), may hold values 0 or 1
- patch_start: int32 [256], P('scen'), parts along dimension 0, may hold values from 0 to 1920
- rad_kernel: bfloat16 [16, 1024, 512], P(None, ('lag', 'elem')), may hold values from -0.0625 to 0.0625
- block_map: int32 [16, 4], P(('lag', 'elem')), may hold values from 0 to 15, all different within a row
Outputs:
- slip_now: float32 [256, 2048], P(('scen', 'lag'), 'elem'), parts along dimension 0
- traction: float32 [256, 2048], P(('scen', 'lag'), 'elem'), parts along dimension 0
- motion: float32 [256, 1024], P('scen', ('lag', 'elem')), parts along dimension 0
The draws below stay inside these ranges and needn't reach their ends.
There are 2 independent parts, one for each index of `scen`. The reference program is written for one: setup_inputs(seed, part) draws one part's arguments, and reference() takes and returns one part's arrays. A program takes and returns all parts, laid end to end along the dimension named above; an argument that names none is the same for every part. Nothing has to cross between parts.
Inputs may be any that keep to these rules, and one draw needn't show every extreme that they name: `block_map`: each row names 4 different source blocks, and every block is named by some row.
All inputs are finite; a program needn't handle non-finite values. No bound on the sum of `cohesive_flags` on one device may be relied on, other than what follows from the above.
Results may differ from the reference program's by a relative error of at most 0.0018.
Values may be sent and summed in bfloat16 or wider, within the bound.
A program may use at most 128 MiB of HBM per device.

```python
import jax
import jax.numpy as jnp
from jax import lax

E = 2048
SCN = 128
L = 16
STEPS = 4
RLAGS = 16
SBLK = 16
EB = 128
NB = 4
RBS = 64
RBLK = 16
R = 1024
PATCH = 128


def set_ends(values, key, smallest, high):
    place = [jax.random.randint(jax.random.fold_in(key, axis), (), 0, length) for axis, length in enumerate(values.shape)]
    main_axis = values.shape.index(max(values.shape))
    beside = place[:main_axis] + [(place[main_axis] + 1) % values.shape[main_axis]] + place[main_axis + 1:]
    return values.at[tuple(place)].set(smallest).at[tuple(beside)].set(high)


def levels(key, dims, cuts, low, largest):
    def one(dim, shards_of):
        steps = jax.random.uniform(jax.random.fold_in(jax.random.fold_in(key, 6), dim), (shards_of,), jnp.float32, low / len(cuts), largest / len(cuts))
        return jnp.repeat(jnp.exp(steps), dims[dim] // shards_of).reshape((-1,) + (1,) * (len(dims) - dim - 1))

    level = one(*cuts[0])
    for cut in cuts[1:]:
        level = level * one(*cut)
    return level


def different_ones(rng, rows, amount, top, lift):
    order = jax.random.permutation(jax.random.fold_in(rng, 1), amount)
    boost = order
    for power in range(3):
        boost = boost * boost // amount
    boost = boost * lift // amount
    tickets = jax.random.randint(jax.random.fold_in(rng, 2), (rows, amount), 0, 4096) + boost
    holders = jax.random.permutation(jax.random.fold_in(rng, 3), rows)[jnp.arange(amount) % rows]
    tickets = jnp.where(jnp.arange(rows)[:, None] == holders[None, :], 1 << 14, tickets)
    score = tickets * amount + jnp.arange(amount)
    return lax.top_k(score.astype(jnp.int32), top)[1].astype(jnp.int32)


def centred(rng, dims, width, reach, cuts=(), kind=jnp.bfloat16):
    drawn = jax.random.normal(rng, dims, jnp.float32) * width
    if len(cuts) > 0:
        drawn = levels(rng, dims, cuts, -0.22, 0.18) * drawn
    return jnp.clip(drawn, min=-reach, max=reach).astype(kind)


def setup_inputs(seed: int = 0, part: int = 0) -> dict:
    key_list = jax.random.split(jax.random.key(seed), 10)
    part_splits = jax.random.split(jax.random.fold_in(key_list[9], part), 10)
    kernel = centred(key_list[0], (L, E, E), (L * E) ** -0.5, 0.03125, ((0, 4), (1, 4)))
    past_rate = jnp.clip(1.0 * jax.random.uniform(part_splits[1], (L, SCN, E), jnp.float32) ** levels(part_splits[1], (L, SCN, E), ((0, 4),), -0.2, 0.2), 0.0, 1.0).astype(jnp.bfloat16)
    loading = centred(part_splits[2], (SCN, E), 1.0, 6.0, ((1, 4),), jnp.float32)
    initial_slip = jnp.clip(1.0 * jax.random.uniform(part_splits[3], (SCN, E), jnp.float32) ** levels(part_splits[3], (SCN, E), ((1, 4),), -0.2, 0.2), 0.0, 1.0)
    peak_strength = jnp.clip(0.5 + 1.5 * jax.random.uniform(key_list[4], (E,), jnp.float32) ** levels(key_list[4], (E,), ((0, 4),), -0.2, 0.2), 0.5, 2.0)
    cohesive_flags = set_ends((jax.random.randint(key_list[5], (E,), 0, 2) < 1).astype(jnp.int32), jax.random.fold_in(key_list[5], 1), 0, 1)
    patch_start = set_ends(jax.random.randint(part_splits[6], (SCN,), 0, E - PATCH + 1), jax.random.fold_in(part_splits[6], 1), 0, E - PATCH).astype(jnp.int32)
    rad_kernel = centred(key_list[7], (RLAGS, R, NB * EB), (RLAGS * NB * EB) ** -0.5, 0.0625, ((1, 16),))
    block_map = different_ones(key_list[8], RBLK, SBLK, NB, 0)
    return dict(kernel=kernel, past_rate=past_rate, loading=loading, initial_slip=initial_slip, peak_strength=peak_strength, cohesive_flags=cohesive_flags, patch_start=patch_start, rad_kernel=rad_kernel, block_map=block_map)


OVERSTRESS = 2.0
WEAKEN = 0.5
CRITICAL = 0.5


def lag_product(history, kernel):
    def add_lag(summed, operands):
        history_row, kernel_slab = operands
        product = jnp.dot(history_row.astype(jnp.float32), kernel_slab.astype(jnp.float32).T, precision=lax.Precision.HIGHEST)
        return summed + product, None

    start_sum = jnp.zeros((history.shape[1], kernel.shape[1]), jnp.float32)
    summed, _ = lax.scan(add_lag, start_sum, (history, kernel))
    return summed


def reference(kernel, past_rate, loading, initial_slip, peak_strength, cohesive_flags, patch_start, rad_kernel, block_map):
    positions = jnp.arange(E, dtype=jnp.int32)[None, :]
    first_cell = patch_start.astype(jnp.int32)[:, None]
    inside = jnp.where((positions >= first_cell) & (positions < first_cell + PATCH), 1.0, 0.0).astype(jnp.float32)
    driven = loading + OVERSTRESS * inside
    weakening = WEAKEN * cohesive_flags.astype(jnp.float32)
    slip_now = initial_slip
    new_rates = []
    traction = driven
    for moment in range(STEPS):
        if moment:
            history = jnp.concatenate([jnp.stack(new_rates[::-1]), past_rate[:L - moment]], 0)
        else:
            history = past_rate
        traction = driven + lag_product(history, kernel)
        strength = peak_strength * (1.0 - weakening * slip_now / (slip_now + CRITICAL))
        slip_rate = jnp.maximum(traction - strength, 0.0).astype(jnp.bfloat16)
        slip_now = slip_now + slip_rate.astype(jnp.float32)
        new_rates.append(slip_rate)
    recent = jnp.concatenate([jnp.stack(new_rates[::-1]), past_rate[:RLAGS - STEPS]], 0)
    grouped = recent.reshape(RLAGS, SCN, SBLK, EB)
    kernels = jnp.moveaxis(rad_kernel.reshape(RLAGS, RBLK, RBS, NB * EB), 1, 0)

    def radiate(operands):
        block_kernel, sources = operands
        chosen = jnp.take(grouped, sources.astype(jnp.int32), axis=2).reshape(RLAGS, SCN, NB * EB)
        return jnp.einsum("msk,mrk->sr", chosen.astype(jnp.float32), block_kernel.astype(jnp.float32), precision=lax.Precision.HIGHEST)

    motion = lax.map(radiate, (kernels, block_map))
    motion = jnp.moveaxis(motion, 0, 1).reshape(SCN, RBLK * RBS)
    return slip_now, traction, motion
```

```python
import functools

import jax
import jax.numpy as jnp
from jax import lax
from jax.experimental import pallas as pl
from jax.experimental.pallas import tpu as pltpu
from jax.sharding import PartitionSpec as P

STEPS = 4
SBLK = 16
PATCH = 128
OVERSTRESS = 2.0
WEAKEN = 0.5
CRITICAL = 0.5

CHUNKS = 2


def flip(e, bits):
    bit = 1
    while bit <= bits:
        if bits & bit:
            e = e + bit - 2 * bit * ((e // bit) % 2)
        bit *= 2
    return e


def nt(a, b):
    return lax.dot_general(a, b, (((1,), (1,)), ((), ())), preferred_element_type=jnp.float32)


def body(
    n_lag, n_elem, near,
    kernel_h, past_h, loading, initial, peak, flags, patch, rad_h, bpad,
    slip_out, trac_out, motion_out,
    kern, hist, rad, radin, bin_v, psum, pin, slip, trs, trin, mpart, min_,
    ksem, psem, rsem,
    z_s, z_r, g_s, g_r, p_s, p_r, v_s, v_r, rad_s, rad_r, bm_s, bm_r, t_s, t_r, m_s, m_r,
):
    depth, cols, _ = kern.shape
    scen = psum.shape[1]
    NEW = STEPS - 1 + depth
    crow = scen // CHUNKS
    rows = scen // n_lag
    handlers = (rad_h.shape[0] - STEPS) // depth
    lag = lax.axis_index("lag")
    elem = lax.axis_index("elem")
    first = lag == 0
    later = lag > 0
    inner = lag < n_lag - 1
    up = lax.rem(lag + 1, n_lag)
    down = lax.rem(lag + n_lag - 1, n_lag)
    bits = []
    bit = n_elem // 2
    while bit:
        bits.append(bit)
        bit //= 2

    pending = []

    def remote(src, dst, ss, rs, **where):
        return pltpu.make_async_remote_copy(
            src_ref=src, dst_ref=dst, send_sem=ss, recv_sem=rs,
            device_id=where, device_id_type=pl.DeviceIdType.MESH)

    def go(desc, cond=None):
        if cond is None:
            desc.start()
        else:
            pl.when(cond)(desc.start)
        pending.append((cond, desc))

    kcopies = [pltpu.make_async_copy(kernel_h.at[i], kern.at[i], ksem.at[i]) for i in range(depth)]
    pcopies = [[pltpu.make_async_copy(past_h.at[i, :, pl.ds(q * cols, cols)], hist.at[STEPS - 1 + i, q], psem.at[i, q])
                for q in range(n_elem)] for i in range(depth)]
    rcopy = pltpu.make_async_copy(rad_h, rad, rsem)
    for i in range(depth):
        for c in pcopies[i]:
            c.start()
        kcopies[i].start()
    rcopy.start()

    barrier = pltpu.get_barrier_semaphore()

    def greet(k, c):
        pl.semaphore_signal(barrier, inc=1, device_id={"lag": lax.rem(lag + k, n_lag)},
                            device_id_type=pl.DeviceIdType.MESH)
        return c

    lax.fori_loop(1, n_lag, greet, 0)
    for b in bits:
        pl.semaphore_signal(barrier, inc=1, device_id={"elem": flip(elem, b)},
                            device_id_type=pl.DeviceIdType.MESH)
    pl.semaphore_wait(barrier, n_lag - 1 + len(bits))

    def stages():
        held = [0]
        out = []
        for b in bits:
            out.append((b, list(held)))
            held = held + [h ^ b for h in held]
        return out

    plan = stages()

    def g_desc(slot, k, n, off):
        b = plan[k][0]
        q = flip(elem, off)
        return remote(hist.at[slot, q], hist.at[slot, q], g_s.at[slot, k, n], g_r.at[slot, k, n],
                      elem=flip(elem, b))

    def g_start(slot, k, cond=None):
        for n, off in enumerate(plan[k][1]):
            go(g_desc(slot, k, n, off), cond)

    def g_wait(slot, k, cond=None):
        b = plan[k][0]

        def act():
            for n, off in enumerate(plan[k][1]):
                q = flip(flip(elem, off), b)
                remote(hist.at[slot, q], hist.at[slot, q], g_s.at[slot, k, n], g_r.at[slot, k, n],
                       elem=flip(elem, b)).wait_recv()
        act() if cond is None else pl.when(cond)(act)

    last = len(bits) - 1

    def g_rest(slot, cond=None):
        for k in range(len(bits)):
            g_wait(slot, k, cond)
            if k < last:
                g_start(slot, k + 1, cond)

    def z_desc(j):
        slot = STEPS - 2 - j
        return remote(past_h.at[depth - 1 - j, :, pl.ds(pl.multiple_of(elem * cols, cols), cols)],
                      hist.at[slot, elem], z_s.at[j], z_r.at[j], lag=up)

    for j in range(STEPS - 1):
        go(z_desc(j), inner)

    def mm(slot, i):
        acc = None
        for q in range(n_elem):
            term = nt(hist[slot, q], kern[i, :, q * cols:(q + 1) * cols])
            acc = term if acc is None else acc + term
        return acc

    lane = lax.broadcasted_iota(jnp.int32, (scen, cols), 1) + elem * cols
    begin = patch[...]
    weakening = WEAKEN * flags[...].astype(jnp.float32)

    @pl.when(first)
    def _():
        slip[...] = initial[...]

    def v_desc(t, c):
        part = hist.at[NEW + t, elem, pl.ds(c * crow, crow), :]
        return remote(part, part, v_s.at[t, c], v_r.at[t, c], lag=up)

    def relay_rate(t):
        for c in range(CHUNKS):
            pl.when(later)(v_desc(t, c).wait_recv)
            go(v_desc(t, c), inner & later)
        g_start(NEW + t, 0, later)

    for t in range(STEPS):
        acc = None
        for i in range(t, depth):
            if t == 0:
                for c in pcopies[i]:
                    c.wait()
                kcopies[i].wait()
            term = mm(STEPS - 1 + i - t, i)
            acc = term if acc is None else acc + term
        for i in range(1, t):
            acc = acc + mm(jnp.where(first, NEW + t - 1 - i, STEPS - 1 + i - t), i)
        psum[t] = acc
        if t:
            slot = STEPS - 1 - t
            g_rest(slot, later)
            g_rest(NEW + t - 1, first)
            psum[t] += mm(jnp.where(first, NEW + t - 1, slot), 0)
        if t < STEPS - 1:
            pl.when(later)(z_desc(t).wait_recv)
            g_start(STEPS - 2 - t, 0, later)
        for c in range(CHUNKS):
            span = pl.ds(c * crow, crow)

            def chain(c=c, span=span, t=t):
                remote(psum.at[t, span, :], pin.at[t, span, :], p_s.at[t, c], p_r.at[t, c], lag=down).wait_recv()
                psum[t, span, :] += pin[t, span, :]
            pl.when(inner)(chain)
            go(remote(psum.at[t, span, :], pin.at[t, span, :], p_s.at[t, c], p_r.at[t, c], lag=down), later)

        @pl.when(first)
        def _(t=t):
            inside = jnp.where((lane >= begin) & (lane < begin + PATCH), 1.0, 0.0).astype(jnp.float32)
            traction = loading[...] + OVERSTRESS * inside + psum[t]
            now = slip[...]
            strength = peak[...] * (1.0 - weakening * now / (now + CRITICAL))
            rate = jnp.maximum(traction - strength, 0.0).astype(jnp.bfloat16)
            slip[...] = now + rate.astype(jnp.float32)
            hist[NEW + t, elem] = rate
            if t == STEPS - 1:
                for d in range(n_lag):
                    trs[d] = traction[d * rows:(d + 1) * rows]
        g_start(NEW + t, 0, first)
        for c in range(CHUNKS):
            go(v_desc(t, c), first & inner)

        if t == 0:
            for h in range(handlers):
                go(remote(rad_h.at[pl.ds(STEPS + h * depth, depth)], radin.at[lag],
                          rad_s.at[h], rad_r.at[lag], lag=h), lag != h)
                go(remote(bpad, bin_v.at[lag], bm_s.at[h], bm_r.at[lag], lag=h), lag != h)
        if t >= 2:
            relay_rate(t - 2)
    for t in range(2, STEPS):
        relay_rate(t)

    def t_desc(k):
        d = lax.rem(lag + k, n_lag)
        return remote(trs.at[d], trin, t_s.at[d], t_r, lag=d)

    @pl.when(first)
    def _():
        lax.fori_loop(1, n_lag, lambda k, c: (t_desc(k).start(), c)[1], 0)

    rcopy.wait()

    recv = motion_out.shape[0]
    width = kernel_h.shape[2] // SBLK
    per = cols // width

    def radiate(kernels, slots, blocks):
        masks = [[jnp.broadcast_to(blocks[0:1, k:k + 1], (recv, width)) == b for k in range(near)]
                 for b in range(SBLK)]
        acc = jnp.zeros((recv, scen), jnp.float32)
        for get, slot in zip(kernels, slots):
            value = get().astype(jnp.float32)
            for q in range(n_elem):
                spread = []
                for b in range(q * per, (q + 1) * per):
                    block = jnp.zeros((recv, width), jnp.float32)
                    for k in range(near):
                        block = jnp.where(masks[b][k], value[:, k * width:(k + 1) * width], block)
                    spread.append(block)
                acc = acc + nt(jnp.concatenate(spread, axis=1).astype(jnp.bfloat16), hist[slot, q])
        return acc

    @pl.when(lag < handlers)
    def _():
        def one(k, c):
            d = lax.rem(lag + k, n_lag)
            remote(rad_h.at[pl.ds(0, depth)], radin.at[d], rad_s.at[0], rad_r.at[d], lag=0).wait_recv()
            remote(bpad, bin_v.at[d], bm_s.at[0], bm_r.at[d], lag=0).wait_recv()
            mpart[d] = radiate([lambda j=j: radin[d, j] for j in range(depth)],
                               [STEPS - 1 + j for j in range(depth)], bin_v[d])
            remote(mpart.at[d], min_.at[lag], m_s.at[d], m_r.at[lag], lag=d).start()
            return c
        lax.fori_loop(1, n_lag, one, 0)
        min_[lag] = radiate([lambda j=j: rad[STEPS + lag * depth + j] for j in range(depth)],
                            [STEPS - 1 + j for j in range(depth)], bpad[...])

    for t in range(STEPS):
        cond = later if t < STEPS - 1 else None
        g_rest(NEW + t, cond)
    motion_out[...] = radiate([lambda m=m: rad[m] for m in range(STEPS)],
                              [NEW + STEPS - 1 - m for m in range(STEPS)], bpad[...])

    whole = initial[...]
    for t in range(STEPS):
        whole = whole + hist[NEW + t, elem].astype(jnp.float32)
    for d in range(n_lag):
        @pl.when(lag == d)
        def _(d=d):
            slip_out[...] = whole[d * rows:(d + 1) * rows]

    @pl.when(first)
    def _():
        trac_out[...] = trs[0]

    @pl.when(later)
    def _():
        remote(trs.at[0], trin, t_s.at[0], t_r, lag=0).wait_recv()
        trac_out[...] = trin[...]

    for h in range(handlers):
        @pl.when(lag != h)
        def _(h=h):
            remote(mpart.at[0], min_.at[h], m_s.at[0], m_r.at[h], lag=h).wait_recv()
        motion_out[...] += min_[h]

    for cond, desc in pending:
        if cond is None:
            desc.wait_send()
        else:
            pl.when(cond)(desc.wait_send)

    @pl.when(first)
    def _():
        lax.fori_loop(1, n_lag, lambda k, c: (t_desc(k).wait_send(), c)[1], 0)

    @pl.when(lag < handlers)
    def _():
        def one(k, c):
            d = lax.rem(lag + k, n_lag)
            remote(mpart.at[d], min_.at[lag], m_s.at[d], m_r.at[lag], lag=d).wait_send()
            return c
        lax.fori_loop(1, n_lag, one, 0)


def on_device(n_lag, n_elem, kernel, past_rate, loading, initial_slip, peak_strength, cohesive_flags, patch_start,
              rad_kernel, block_map):
    depth, cols, _ = kernel.shape
    scen = past_rate.shape[1]
    lags, recv, wide = rad_kernel.shape
    rows = scen // n_lag
    handlers = (lags - STEPS) // depth
    nbits = n_elem.bit_length() - 1
    bpad = jnp.zeros((8, 128), jnp.int32).at[:1, :block_map.shape[1]].set(block_map)
    f32, bf16 = jnp.float32, jnp.bfloat16
    dma = pltpu.SemaphoreType.DMA
    vmem = pl.BlockSpec(memory_space=pltpu.VMEM)
    hbm = pl.BlockSpec(memory_space=pl.ANY)
    slots = 2 * STEPS - 1 + depth
    slip, traction, motion = pl.pallas_call(
        functools.partial(body, n_lag, n_elem, block_map.shape[1]),
        out_shape=(
            jax.ShapeDtypeStruct((rows, cols), f32),
            jax.ShapeDtypeStruct((rows, cols), f32),
            jax.ShapeDtypeStruct((recv, scen), f32),
        ),
        in_specs=[hbm, hbm, vmem, vmem, vmem, vmem, vmem, hbm, vmem],
        out_specs=(vmem, vmem, vmem),
        scratch_shapes=[
            pltpu.VMEM((depth, cols, kernel.shape[2]), bf16),
            pltpu.VMEM((slots, n_elem, scen, cols), bf16),
            pltpu.VMEM((lags, recv, wide), bf16),
            pltpu.VMEM((n_lag, depth, recv, wide), bf16),
            pltpu.VMEM((n_lag, 8, 128), jnp.int32),
            pltpu.VMEM((STEPS, scen, cols), f32),
            pltpu.VMEM((STEPS, scen, cols), f32),
            pltpu.VMEM((scen, cols), f32),
            pltpu.VMEM((n_lag, rows, cols), f32),
            pltpu.VMEM((rows, cols), f32),
            pltpu.VMEM((n_lag, recv, scen), f32),
            pltpu.VMEM((max(handlers, 1), recv, scen), f32),
            dma((depth,)), dma((depth, n_elem)), dma,
            dma((STEPS,)), dma((STEPS,)),
            dma((slots, nbits, n_elem)), dma((slots, nbits, n_elem)),
            dma((STEPS, CHUNKS)), dma((STEPS, CHUNKS)),
            dma((STEPS, CHUNKS)), dma((STEPS, CHUNKS)),
            dma((handlers,)), dma((n_lag,)),
            dma((handlers,)), dma((n_lag,)),
            dma((n_lag,)), dma,
            dma((n_lag,)), dma((n_lag,)),
        ],
        compiler_params=pltpu.CompilerParams(
            collective_id=0, has_side_effects=True, vmem_limit_bytes=60 * 1024 * 1024),
    )(kernel, past_rate, loading, initial_slip, peak_strength[None], cohesive_flags[None], patch_start[:, None],
      rad_kernel, bpad)
    return slip, traction, motion.T


def solution(mesh):
    n_lag, n_elem = mesh.shape["lag"], mesh.shape["elem"]
    return jax.shard_map(
        functools.partial(on_device, n_lag, n_elem),
        mesh=mesh,
        in_specs=(
            P("lag", "elem", None),
            P("lag", "scen", None),
            P("scen", "elem"),
            P("scen", "elem"),
            P("elem"),
            P("elem"),
            P("scen"),
            P(None, ("lag", "elem"), None),
            P(("lag", "elem"), None),
        ),
        out_specs=(
            P(("scen", "lag"), "elem"),
            P(("scen", "lag"), "elem"),
            P("scen", ("lag", "elem")),
        ),
        check_vma=False,
    )
```

```python
import functools

import jax
import jax.numpy as jnp
from jax import lax
from jax.experimental import pallas as pl
from jax.experimental.pallas import tpu as pltpu
from jax.sharding import PartitionSpec as P

STEPS = 4
SBLK = 16
PATCH = 128
OVERSTRESS = 2.0
WEAKEN = 0.5
CRITICAL = 0.5

CHUNKS = 4
LEVELS = 32767.0


def flip(e, bits):
    bit = 1
    while bit <= bits:
        if bits & bit:
            e = e + bit - 2 * bit * ((e // bit) % 2)
        bit *= 2
    return e


def nt(a, b):
    return lax.dot_general(a, b, (((1,), (1,)), ((), ())), preferred_element_type=jnp.float32)


def body(
    n_lag, n_elem, near,
    kernel_h, past_h, loading, initial, peak, flags, patch, rad_h, bpad,
    slip_out, trac_out, motion_out,
    kern, hist, rad, radin, bin_v, psum, pout, pin, sout, sin, slip, trs, trin, mpart, min_,
    ksem, psem, rsem,
    z_s, z_r, g_s, g_r, p_s, p_r, q_s, q_r, v_s, v_r, rad_s, rad_r, bm_s, bm_r, t_s, t_r, m_s, m_r,
):
    depth, cols, _ = kern.shape
    scen = psum.shape[1]
    NEW = STEPS - 1 + depth
    crow = scen // CHUNKS
    rows = scen // n_lag
    handlers = (rad_h.shape[0] - STEPS) // depth
    lag = lax.axis_index("lag")
    elem = lax.axis_index("elem")
    first = lag == 0
    later = lag > 0
    inner = lag < n_lag - 1
    up = lax.rem(lag + 1, n_lag)
    down = lax.rem(lag + n_lag - 1, n_lag)
    bits = []
    bit = n_elem // 2
    while bit:
        bits.append(bit)
        bit //= 2

    pending = []

    def remote(src, dst, ss, rs, **where):
        return pltpu.make_async_remote_copy(
            src_ref=src, dst_ref=dst, send_sem=ss, recv_sem=rs,
            device_id=where, device_id_type=pl.DeviceIdType.MESH)

    def go(desc, cond=None):
        if cond is None:
            desc.start()
        else:
            pl.when(cond)(desc.start)
        pending.append((cond, desc))

    kcopies = [pltpu.make_async_copy(kernel_h.at[i], kern.at[i], ksem.at[i]) for i in range(depth)]
    pcopies = [[pltpu.make_async_copy(past_h.at[i, :, pl.ds(q * cols, cols)], hist.at[STEPS - 1 + i, q], psem.at[i, q])
                for q in range(n_elem)] for i in range(depth)]
    rcopy = pltpu.make_async_copy(rad_h, rad, rsem)
    for i in range(depth):
        for c in pcopies[i]:
            c.start()
        kcopies[i].start()
    rcopy.start()

    barrier = pltpu.get_barrier_semaphore()

    def greet(k, c):
        pl.semaphore_signal(barrier, inc=1, device_id={"lag": lax.rem(lag + k, n_lag)},
                            device_id_type=pl.DeviceIdType.MESH)
        return c

    lax.fori_loop(1, n_lag, greet, 0)
    for b in bits:
        pl.semaphore_signal(barrier, inc=1, device_id={"elem": flip(elem, b)},
                            device_id_type=pl.DeviceIdType.MESH)
    pl.semaphore_wait(barrier, n_lag - 1 + len(bits))

    def stages():
        held = [0]
        out = []
        for b in bits:
            out.append((b, list(held)))
            held = held + [h ^ b for h in held]
        return out

    plan = stages()

    def g_desc(slot, k, n, off):
        b = plan[k][0]
        q = flip(elem, off)
        return remote(hist.at[slot, q], hist.at[slot, q], g_s.at[slot, k, n], g_r.at[slot, k, n],
                      elem=flip(elem, b))

    def g_start(slot, k, cond=None):
        for n, off in enumerate(plan[k][1]):
            go(g_desc(slot, k, n, off), cond)

    def g_wait(slot, k, cond=None):
        b = plan[k][0]

        def act():
            for n, off in enumerate(plan[k][1]):
                q = flip(flip(elem, off), b)
                remote(hist.at[slot, q], hist.at[slot, q], g_s.at[slot, k, n], g_r.at[slot, k, n],
                       elem=flip(elem, b)).wait_recv()
        act() if cond is None else pl.when(cond)(act)

    last = len(bits) - 1

    def g_rest(slot, cond=None):
        for k in range(len(bits)):
            g_wait(slot, k, cond)
            if k < last:
                g_start(slot, k + 1, cond)

    def z_desc(j):
        slot = STEPS - 2 - j
        return remote(past_h.at[depth - 1 - j, :, pl.ds(pl.multiple_of(elem * cols, cols), cols)],
                      hist.at[slot, elem], z_s.at[j], z_r.at[j], lag=up)

    for j in range(STEPS - 1):
        go(z_desc(j), inner)

    def mm(slot, i):
        acc = None
        for q in range(n_elem):
            term = nt(hist[slot, q], kern[i, :, q * cols:(q + 1) * cols])
            acc = term if acc is None else acc + term
        return acc

    lane = lax.broadcasted_iota(jnp.int32, (scen, cols), 1) + elem * cols
    begin = patch[...]
    weakening = WEAKEN * flags[...].astype(jnp.float32)

    @pl.when(first)
    def _():
        slip[...] = initial[...]

    def v_desc(t, c):
        part = hist.at[NEW + t, elem, pl.ds(c * crow, crow), :]
        return remote(part, part, v_s.at[t, c], v_r.at[t, c], lag=up)

    def relay_rate(t):
        for c in range(CHUNKS):
            pl.when(later)(v_desc(t, c).wait_recv)
            go(v_desc(t, c), inner & later)
        g_start(NEW + t, 0, later)

    for t in range(STEPS):
        acc = None
        for i in range(t, depth):
            if t == 0:
                for c in pcopies[i]:
                    c.wait()
                kcopies[i].wait()
            term = mm(STEPS - 1 + i - t, i)
            acc = term if acc is None else acc + term
        for i in range(1, t):
            acc = acc + mm(jnp.where(first, NEW + t - 1 - i, STEPS - 1 + i - t), i)
        psum[t] = acc
        if t:
            slot = STEPS - 1 - t
            g_rest(slot, later)
            g_rest(NEW + t - 1, first)
            psum[t] += mm(jnp.where(first, NEW + t - 1, slot), 0)
        if t < STEPS - 1:
            pl.when(later)(z_desc(t).wait_recv)
            g_start(STEPS - 2 - t, 0, later)
        for c in range(CHUNKS):
            span = pl.ds(c * crow, crow)

            def moves(c=c, span=span, t=t):
                return (remote(pout.at[t, span, :], pin.at[t, span, :], p_s.at[t, c], p_r.at[t, c], lag=down),
                        remote(sout.at[t, c], sin.at[t, c], q_s.at[t, c], q_r.at[t, c], lag=down))

            @pl.when(inner)
            def _(moves=moves, c=c, span=span, t=t):
                for move in moves():
                    move.wait_recv()
                psum[t, span, :] += pin[t, span, :].astype(jnp.int32).astype(jnp.float32) * sin[t, c, 0:1, 0:1]

            @pl.when(later)
            def _(c=c, span=span, t=t):
                value = psum[t, span, :]
                top = jnp.maximum(jnp.max(jnp.abs(value), axis=(0, 1), keepdims=True), 1e-30)
                pout[t, span, :] = jnp.floor(value * (LEVELS / top) + 0.5).astype(jnp.int32).astype(jnp.int16)
                sout[t, c] = jnp.broadcast_to(top / LEVELS, sout.shape[2:])
            for move in moves():
                go(move, later)

        @pl.when(first)
        def _(t=t):
            inside = jnp.where((lane >= begin) & (lane < begin + PATCH), 1.0, 0.0).astype(jnp.float32)
            traction = loading[...] + OVERSTRESS * inside + psum[t]
            now = slip[...]
            strength = peak[...] * (1.0 - weakening * now / (now + CRITICAL))
            rate = jnp.maximum(traction - strength, 0.0).astype(jnp.bfloat16)
            slip[...] = now + rate.astype(jnp.float32)
            hist[NEW + t, elem] = rate
            if t == STEPS - 1:
                for d in range(n_lag):
                    trs[d] = traction[d * rows:(d + 1) * rows]
        g_start(NEW + t, 0, first)
        for c in range(CHUNKS):
            go(v_desc(t, c), first & inner)

        if t == 0:
            for h in range(handlers):
                go(remote(rad_h.at[pl.ds(STEPS + h * depth, depth)], radin.at[lag],
                          rad_s.at[h], rad_r.at[lag], lag=h), lag != h)
                go(remote(bpad, bin_v.at[lag], bm_s.at[h], bm_r.at[lag], lag=h), lag != h)
        if t >= 2:
            relay_rate(t - 2)
    for t in range(2, STEPS):
        relay_rate(t)

    def t_desc(k):
        d = lax.rem(lag + k, n_lag)
        return remote(trs.at[d], trin, t_s.at[d], t_r, lag=d)

    @pl.when(first)
    def _():
        lax.fori_loop(1, n_lag, lambda k, c: (t_desc(k).start(), c)[1], 0)

    rcopy.wait()

    recv = motion_out.shape[0]
    width = kernel_h.shape[2] // SBLK
    per = cols // width

    def radiate(kernels, slots, blocks):
        masks = [[jnp.broadcast_to(blocks[0:1, k:k + 1], (recv, width)) == b for k in range(near)]
                 for b in range(SBLK)]
        acc = jnp.zeros((recv, scen), jnp.float32)
        for get, slot in zip(kernels, slots):
            value = get().astype(jnp.float32)
            for q in range(n_elem):
                spread = []
                for b in range(q * per, (q + 1) * per):
                    block = jnp.zeros((recv, width), jnp.float32)
                    for k in range(near):
                        block = jnp.where(masks[b][k], value[:, k * width:(k + 1) * width], block)
                    spread.append(block)
                acc = acc + nt(jnp.concatenate(spread, axis=1).astype(jnp.bfloat16), hist[slot, q])
        return acc

    @pl.when(lag < handlers)
    def _():
        def one(k, c):
            d = lax.rem(lag + k, n_lag)
            remote(rad_h.at[pl.ds(0, depth)], radin.at[d], rad_s.at[0], rad_r.at[d], lag=0).wait_recv()
            remote(bpad, bin_v.at[d], bm_s.at[0], bm_r.at[d], lag=0).wait_recv()
            mpart[d] = radiate([lambda j=j: radin[d, j] for j in range(depth)],
                               [STEPS - 1 + j for j in range(depth)], bin_v[d])
            remote(mpart.at[d], min_.at[lag], m_s.at[d], m_r.at[lag], lag=d).start()
            return c
        lax.fori_loop(1, n_lag, one, 0)
        min_[lag] = radiate([lambda j=j: rad[STEPS + lag * depth + j] for j in range(depth)],
                            [STEPS - 1 + j for j in range(depth)], bpad[...])

    for t in range(STEPS):
        cond = later if t < STEPS - 1 else None
        g_rest(NEW + t, cond)
    motion_out[...] = radiate([lambda m=m: rad[m] for m in range(STEPS)],
                              [NEW + STEPS - 1 - m for m in range(STEPS)], bpad[...])

    whole = initial[...]
    for t in range(STEPS):
        whole = whole + hist[NEW + t, elem].astype(jnp.float32)
    for d in range(n_lag):
        @pl.when(lag == d)
        def _(d=d):
            slip_out[...] = whole[d * rows:(d + 1) * rows]

    @pl.when(first)
    def _():
        trac_out[...] = trs[0]

    @pl.when(later)
    def _():
        remote(trs.at[0], trin, t_s.at[0], t_r, lag=0).wait_recv()
        trac_out[...] = trin[...]

    for h in range(handlers):
        @pl.when(lag != h)
        def _(h=h):
            remote(mpart.at[0], min_.at[h], m_s.at[0], m_r.at[h], lag=h).wait_recv()
        motion_out[...] += min_[h]

    for cond, desc in pending:
        if cond is None:
            desc.wait_send()
        else:
            pl.when(cond)(desc.wait_send)

    @pl.when(first)
    def _():
        lax.fori_loop(1, n_lag, lambda k, c: (t_desc(k).wait_send(), c)[1], 0)

    @pl.when(lag < handlers)
    def _():
        def one(k, c):
            d = lax.rem(lag + k, n_lag)
            remote(mpart.at[d], min_.at[lag], m_s.at[d], m_r.at[lag], lag=d).wait_send()
            return c
        lax.fori_loop(1, n_lag, one, 0)


def on_device(n_lag, n_elem, kernel, past_rate, loading, initial_slip, peak_strength, cohesive_flags, patch_start,
              rad_kernel, block_map):
    depth, cols, _ = kernel.shape
    scen = past_rate.shape[1]
    lags, recv, wide = rad_kernel.shape
    rows = scen // n_lag
    handlers = (lags - STEPS) // depth
    nbits = n_elem.bit_length() - 1
    bpad = jnp.zeros((8, 128), jnp.int32).at[:1, :block_map.shape[1]].set(block_map)
    f32, bf16 = jnp.float32, jnp.bfloat16
    dma = pltpu.SemaphoreType.DMA
    vmem = pl.BlockSpec(memory_space=pltpu.VMEM)
    hbm = pl.BlockSpec(memory_space=pl.ANY)
    slots = 2 * STEPS - 1 + depth
    slip, traction, motion = pl.pallas_call(
        functools.partial(body, n_lag, n_elem, block_map.shape[1]),
        out_shape=(
            jax.ShapeDtypeStruct((rows, cols), f32),
            jax.ShapeDtypeStruct((rows, cols), f32),
            jax.ShapeDtypeStruct((recv, scen), f32),
        ),
        in_specs=[hbm, hbm, vmem, vmem, vmem, vmem, vmem, hbm, vmem],
        out_specs=(vmem, vmem, vmem),
        scratch_shapes=[
            pltpu.VMEM((depth, cols, kernel.shape[2]), bf16),
            pltpu.VMEM((slots, n_elem, scen, cols), bf16),
            pltpu.VMEM((lags, recv, wide), bf16),
            pltpu.VMEM((n_lag, depth, recv, wide), bf16),
            pltpu.VMEM((n_lag, 8, 128), jnp.int32),
            pltpu.VMEM((STEPS, scen, cols), f32),
            pltpu.VMEM((STEPS, scen, cols), jnp.int16),
            pltpu.VMEM((STEPS, scen, cols), jnp.int16),
            pltpu.VMEM((STEPS, CHUNKS, 8, 128), f32),
            pltpu.VMEM((STEPS, CHUNKS, 8, 128), f32),
            pltpu.VMEM((scen, cols), f32),
            pltpu.VMEM((n_lag, rows, cols), f32),
            pltpu.VMEM((rows, cols), f32),
            pltpu.VMEM((n_lag, recv, scen), f32),
            pltpu.VMEM((max(handlers, 1), recv, scen), f32),
            dma((depth,)), dma((depth, n_elem)), dma,
            dma((STEPS,)), dma((STEPS,)),
            dma((slots, nbits, n_elem)), dma((slots, nbits, n_elem)),
            dma((STEPS, CHUNKS)), dma((STEPS, CHUNKS)),
            dma((STEPS, CHUNKS)), dma((STEPS, CHUNKS)),
            dma((STEPS, CHUNKS)), dma((STEPS, CHUNKS)),
            dma((handlers,)), dma((n_lag,)),
            dma((handlers,)), dma((n_lag,)),
            dma((n_lag,)), dma,
            dma((n_lag,)), dma((n_lag,)),
        ],
        compiler_params=pltpu.CompilerParams(
            collective_id=0, has_side_effects=True, vmem_limit_bytes=60 * 1024 * 1024),
    )(kernel, past_rate, loading, initial_slip, peak_strength[None], cohesive_flags[None], patch_start[:, None],
      rad_kernel, bpad)
    return slip, traction, motion.T


def solution(mesh):
    n_lag, n_elem = mesh.shape["lag"], mesh.shape["elem"]
    return jax.shard_map(
        functools.partial(on_device, n_lag, n_elem),
        mesh=mesh,
        in_specs=(
            P("lag", "elem", None),
            P("lag", "scen", None),
            P("scen", "elem"),
            P("scen", "elem"),
            P("elem"),
            P("elem"),
            P("scen"),
            P(None, ("lag", "elem"), None),
            P(("lag", "elem"), None),
        ),
        out_specs=(
            P(("scen", "lag"), "elem"),
            P(("scen", "lag"), "elem"),
            P("scen", ("lag", "elem")),
        ),
        check_vma=False,
    )
```

```python
import functools

import jax
import jax.numpy as jnp
from jax import lax
from jax.experimental import pallas as pl
from jax.experimental.pallas import tpu as pltpu
from jax.sharding import PartitionSpec as P

STEPS = 4
SBLK = 16
PATCH = 128
OVERSTRESS = 2.0
WEAKEN = 0.5
CRITICAL = 0.5

CHUNKS = 4
LEVELS = 32767.0


def flip(e, bits):
    bit = 1
    while bit <= bits:
        if bits & bit:
            e = e + bit - 2 * bit * ((e // bit) % 2)
        bit *= 2
    return e


def nt(a, b):
    return lax.dot_general(a, b, (((1,), (1,)), ((), ())), preferred_element_type=jnp.float32)


def body(
    n_lag, n_elem, n_scen, near,
    kernel_h, past_h, loading, initial, peak, flags, patch, rad_h, bpad,
    slip_out, trac_out, motion_out,
    kern, hist, rad, radin, bin_v, psum, pout, pin, sout, sin, slip, trs, trin, rrs, rrin, rz, mpart, min_,
    ksem, psem, rsem,
    z_s, z_r, g_s, g_r, p_s, p_r, q_s, q_r, v_s, v_r, rad_s, rad_r, bm_s, bm_r, t_s, t_r, m_s, m_r, r_s, r_r, rz_s, rz_r, y_s, y_r,
):
    depth, cols, _ = kern.shape
    scen = psum.shape[1]
    NEW = STEPS - 1 + depth
    crow = scen // CHUNKS
    rows = scen // n_lag
    handlers = (rad_h.shape[0] - STEPS) // depth
    lag = lax.axis_index("lag")
    elem = lax.axis_index("elem")
    scn = lax.axis_index("scen")
    other = lax.rem(scn + 1, n_scen)
    half = depth // n_scen
    first = lag == 0
    later = lag > 0
    inner = lag < n_lag - 1
    up = lax.rem(lag + 1, n_lag)
    down = lax.rem(lag + n_lag - 1, n_lag)
    bits = []
    bit = n_elem // 2
    while bit:
        bits.append(bit)
        bit //= 2

    pending = []

    def remote(src, dst, ss, rs, **where):
        return pltpu.make_async_remote_copy(
            src_ref=src, dst_ref=dst, send_sem=ss, recv_sem=rs,
            device_id=where, device_id_type=pl.DeviceIdType.MESH)

    def go(desc, cond=None):
        if cond is None:
            desc.start()
        else:
            pl.when(cond)(desc.start)
        pending.append((cond, desc))

    kcopies = [pltpu.make_async_copy(kernel_h.at[i], kern.at[i], ksem.at[i]) for i in range(depth)]
    pcopies = [[pltpu.make_async_copy(past_h.at[i, :, pl.ds(q * cols, cols)], hist.at[STEPS - 1 + i, q], psem.at[i, q])
                for q in range(n_elem)] for i in range(depth)]
    rcopy = pltpu.make_async_copy(rad_h, rad, rsem)
    for i in range(depth):
        for c in pcopies[i]:
            c.start()
        kcopies[i].start()
    rcopy.start()

    barrier = pltpu.get_barrier_semaphore()

    def greet(k, c):
        pl.semaphore_signal(barrier, inc=1, device_id={"lag": lax.rem(lag + k, n_lag)},
                            device_id_type=pl.DeviceIdType.MESH)
        return c

    lax.fori_loop(1, n_lag, greet, 0)
    for b in bits:
        pl.semaphore_signal(barrier, inc=1, device_id={"elem": flip(elem, b)},
                            device_id_type=pl.DeviceIdType.MESH)
    pl.semaphore_signal(barrier, inc=1, device_id={"scen": other}, device_id_type=pl.DeviceIdType.MESH)
    pl.semaphore_wait(barrier, n_lag + len(bits))

    def stages():
        held = [0]
        out = []
        for b in bits:
            out.append((b, list(held)))
            held = held + [h ^ b for h in held]
        return out

    plan = stages()

    def g_desc(slot, k, n, off):
        b = plan[k][0]
        q = flip(elem, off)
        return remote(hist.at[slot, q], hist.at[slot, q], g_s.at[slot, k, n], g_r.at[slot, k, n],
                      elem=flip(elem, b))

    def g_start(slot, k, cond=None):
        for n, off in enumerate(plan[k][1]):
            go(g_desc(slot, k, n, off), cond)

    def g_wait(slot, k, cond=None):
        b = plan[k][0]

        def act():
            for n, off in enumerate(plan[k][1]):
                q = flip(flip(elem, off), b)
                remote(hist.at[slot, q], hist.at[slot, q], g_s.at[slot, k, n], g_r.at[slot, k, n],
                       elem=flip(elem, b)).wait_recv()
        act() if cond is None else pl.when(cond)(act)

    last = len(bits) - 1

    def g_rest(slot, cond=None):
        for k in range(len(bits)):
            g_wait(slot, k, cond)
            if k < last:
                g_start(slot, k + 1, cond)

    def z_desc(j):
        slot = STEPS - 2 - j
        return remote(past_h.at[depth - 1 - j, :, pl.ds(pl.multiple_of(elem * cols, cols), cols)],
                      hist.at[slot, elem], z_s.at[j], z_r.at[j], lag=up)

    for j in range(STEPS - 1):
        go(z_desc(j), inner)

    def mm(slot, i):
        acc = None
        for q in range(n_elem):
            term = nt(hist[slot, q], kern[i, :, q * cols:(q + 1) * cols])
            acc = term if acc is None else acc + term
        return acc

    lane = lax.broadcasted_iota(jnp.int32, (scen, cols), 1) + elem * cols
    begin = patch[...]
    weakening = WEAKEN * flags[...].astype(jnp.float32)

    @pl.when(first)
    def _():
        slip[...] = initial[...]

    def v_desc(t, c):
        part = hist.at[NEW + t, elem, pl.ds(c * crow, crow), :]
        return remote(part, part, v_s.at[t, c], v_r.at[t, c], lag=up)

    def relay_rate(t):
        for c in range(CHUNKS):
            pl.when(later)(v_desc(t, c).wait_recv)
            go(v_desc(t, c), inner & later)
        g_start(NEW + t, 0, later)

    for t in range(STEPS):
        acc = None
        for i in range(t, depth):
            if t == 0:
                for c in pcopies[i]:
                    c.wait()
                kcopies[i].wait()
            term = mm(STEPS - 1 + i - t, i)
            acc = term if acc is None else acc + term
        for i in range(1, t):
            acc = acc + mm(jnp.where(first, NEW + t - 1 - i, STEPS - 1 + i - t), i)
        psum[t] = acc
        if t:
            slot = STEPS - 1 - t
            g_rest(slot, later)
            g_rest(NEW + t - 1, first)
            psum[t] += mm(jnp.where(first, NEW + t - 1, slot), 0)
        if t < STEPS - 1:
            pl.when(later)(z_desc(t).wait_recv)
            g_start(STEPS - 2 - t, 0, later)
        for c in range(CHUNKS):
            span = pl.ds(c * crow, crow)

            def moves(c=c, span=span, t=t):
                return (remote(pout.at[t, span, :], pin.at[t, span, :], p_s.at[t, c], p_r.at[t, c], lag=down),
                        remote(sout.at[t, c], sin.at[t, c], q_s.at[t, c], q_r.at[t, c], lag=down))

            @pl.when(inner)
            def _(moves=moves, c=c, span=span, t=t):
                for move in moves():
                    move.wait_recv()
                psum[t, span, :] += pin[t, span, :].astype(jnp.int32).astype(jnp.float32) * sin[t, c, 0:1, 0:1]

            @pl.when(later)
            def _(c=c, span=span, t=t):
                value = psum[t, span, :]
                top = jnp.maximum(jnp.max(jnp.abs(value), axis=(0, 1), keepdims=True), 1e-30)
                pout[t, span, :] = jnp.floor(value * (LEVELS / top) + 0.5).astype(jnp.int32).astype(jnp.int16)
                sout[t, c] = jnp.broadcast_to(top / LEVELS, sout.shape[2:])
            for move in moves():
                go(move, later)

        @pl.when(first)
        def _(t=t):
            inside = jnp.where((lane >= begin) & (lane < begin + PATCH), 1.0, 0.0).astype(jnp.float32)
            traction = loading[...] + OVERSTRESS * inside + psum[t]
            now = slip[...]
            strength = peak[...] * (1.0 - weakening * now / (now + CRITICAL))
            rate = jnp.maximum(traction - strength, 0.0).astype(jnp.bfloat16)
            slip[...] = now + rate.astype(jnp.float32)
            hist[NEW + t, elem] = rate
            if t == STEPS - 1:
                for d in range(n_lag):
                    trs[d] = traction[d * rows:(d + 1) * rows]
                    rrs[d] = rate[d * rows:(d + 1) * rows]
        g_start(NEW + t, 0, first)
        if t < STEPS - 1:
            for c in range(CHUNKS):
                go(v_desc(t, c), first & inner)

        if t == 1:
            go(remote(rad_h.at[0], rz.at[lag], rz_s, rz_r.at[lag], lag=0), later)
            for h in range(handlers):
                go(remote(bpad, bin_v.at[lag], bm_s.at[h], bm_r.at[lag], lag=h), lag != h)
                go(remote(rad_h.at[pl.ds(STEPS + h * depth + scn * half, half)],
                          radin.at[lag, pl.ds(scn * half, half)],
                          rad_s.at[h], rad_r.at[lag], lag=h), lag != h)
        if t >= 2:
            relay_rate(t - 2)
    for t in range(2, STEPS - 1):
        relay_rate(t)

    def t_desc(k):
        d = lax.rem(lag + k, n_lag)
        return remote(trs.at[d], trin, t_s.at[d], t_r, lag=d)

    def r_desc(k):
        d = lax.rem(lag + k, n_lag)
        return remote(rrs.at[d], rrin, r_s.at[d], r_r, lag=d)

    def y_desc(d, side):
        part = radin.at[d, pl.ds(side * half, half)]
        return remote(part, part, y_s.at[d], y_r.at[d], scen=other)

    def m_desc(d):
        return remote(mpart.at[d], min_.at[lag], m_s.at[d], m_r.at[lag], lag=d)

    @pl.when(first)
    def _():
        lax.fori_loop(1, n_lag, lambda k, c: (t_desc(k).start(), r_desc(k).start(), c)[2], 0)

    rcopy.wait()

    recv = motion_out.shape[0]
    width = kernel_h.shape[2] // SBLK
    per = cols // width

    def radiate(kernels, slots, blocks):
        masks = [[jnp.broadcast_to(blocks[0:1, k:k + 1], (recv, width)) == b for k in range(near)]
                 for b in range(SBLK)]
        acc = jnp.zeros((recv, scen), jnp.float32)
        for get, slot in zip(kernels, slots):
            value = get().astype(jnp.float32)
            for q in range(n_elem):
                spread = []
                for b in range(q * per, (q + 1) * per):
                    block = jnp.zeros((recv, width), jnp.float32)
                    for k in range(near):
                        block = jnp.where(masks[b][k], value[:, k * width:(k + 1) * width], block)
                    spread.append(block)
                acc = acc + nt(jnp.concatenate(spread, axis=1).astype(jnp.bfloat16), hist[slot, q])
        return acc

    @pl.when(lag < handlers)
    def _():
        def share(k, c):
            d = lax.rem(lag + k, n_lag)
            part = radin.at[d, pl.ds(scn * half, half)]
            remote(part, part, rad_s.at[0], rad_r.at[d], lag=0).wait_recv()
            y_desc(d, scn).start()
            return c
        lax.fori_loop(1, n_lag, share, 0)
        min_[lag] = radiate([lambda j=j: rad[STEPS + lag * depth + j] for j in range(depth)],
                            [STEPS - 1 + j for j in range(depth)], bpad[...])

        def one(k, c):
            d = lax.rem(lag + k, n_lag)
            y_desc(d, other).wait_recv()
            remote(bpad, bin_v.at[d], bm_s.at[0], bm_r.at[d], lag=0).wait_recv()
            mpart[d] = radiate([lambda j=j: radin[d, j] for j in range(depth)],
                               [STEPS - 1 + j for j in range(depth)], bin_v[d])
            pl.when(later)(m_desc(d).start)
            return c
        lax.fori_loop(1, n_lag, one, 0)

    g_rest(NEW + STEPS - 1, first)

    @pl.when(first)
    def _():
        def one(k, c):
            d = lax.rem(lag + k, n_lag)
            remote(rz.at[d], rz.at[d], rz_s, rz_r.at[d], lag=0).wait_recv()
            mpart[d] += radiate([lambda: rz[d]], [NEW + STEPS - 1], bin_v[d])
            m_desc(d).start()
            return c
        lax.fori_loop(1, n_lag, one, 0)
    for t in range(STEPS - 1):
        g_rest(NEW + t, later)
    motion_out[...] = radiate([lambda m=m: rad[m] for m in range(1, STEPS)],
                              [NEW + STEPS - 1 - m for m in range(1, STEPS)], bpad[...])

    @pl.when(first)
    def _():
        motion_out[...] += radiate([lambda: rad[0]], [NEW + STEPS - 1], bpad[...])

    @pl.when(first)
    def _():
        slip_out[...] = slip[0:rows]

    @pl.when(later)
    def _():
        remote(rrs.at[0], rrin, r_s.at[0], r_r, lag=0).wait_recv()
        whole = initial[...]
        for t in range(STEPS - 1):
            whole = whole + hist[NEW + t, elem].astype(jnp.float32)
        for d in range(1, n_lag):
            @pl.when(lag == d)
            def _(d=d):
                slip_out[...] = whole[d * rows:(d + 1) * rows] + rrin[...].astype(jnp.float32)

    @pl.when(first)
    def _():
        trac_out[...] = trs[0]

    @pl.when(later)
    def _():
        remote(trs.at[0], trin, t_s.at[0], t_r, lag=0).wait_recv()
        trac_out[...] = trin[...]

    for h in range(handlers):
        @pl.when(lag != h)
        def _(h=h):
            remote(mpart.at[0], min_.at[h], m_s.at[0], m_r.at[h], lag=h).wait_recv()
        motion_out[...] += min_[h]

    for cond, desc in pending:
        if cond is None:
            desc.wait_send()
        else:
            pl.when(cond)(desc.wait_send)

    @pl.when(first)
    def _():
        lax.fori_loop(1, n_lag, lambda k, c: (t_desc(k).wait_send(), r_desc(k).wait_send(), c)[2], 0)

    @pl.when(lag < handlers)
    def _():
        def one(k, c):
            d = lax.rem(lag + k, n_lag)
            y_desc(d, scn).wait_send()
            m_desc(d).wait_send()
            return c
        lax.fori_loop(1, n_lag, one, 0)


def on_device(n_lag, n_elem, n_scen, kernel, past_rate, loading, initial_slip, peak_strength, cohesive_flags, patch_start,
              rad_kernel, block_map):
    depth, cols, _ = kernel.shape
    scen = past_rate.shape[1]
    lags, recv, wide = rad_kernel.shape
    rows = scen // n_lag
    handlers = (lags - STEPS) // depth
    nbits = n_elem.bit_length() - 1
    bpad = jnp.zeros((8, 128), jnp.int32).at[:1, :block_map.shape[1]].set(block_map)
    f32, bf16 = jnp.float32, jnp.bfloat16
    dma = pltpu.SemaphoreType.DMA
    vmem = pl.BlockSpec(memory_space=pltpu.VMEM)
    hbm = pl.BlockSpec(memory_space=pl.ANY)
    slots = 2 * STEPS - 1 + depth
    slip, traction, motion = pl.pallas_call(
        functools.partial(body, n_lag, n_elem, n_scen, block_map.shape[1]),
        out_shape=(
            jax.ShapeDtypeStruct((rows, cols), f32),
            jax.ShapeDtypeStruct((rows, cols), f32),
            jax.ShapeDtypeStruct((recv, scen), f32),
        ),
        in_specs=[hbm, hbm, vmem, vmem, vmem, vmem, vmem, hbm, vmem],
        out_specs=(vmem, vmem, vmem),
        scratch_shapes=[
            pltpu.VMEM((depth, cols, kernel.shape[2]), bf16),
            pltpu.VMEM((slots, n_elem, scen, cols), bf16),
            pltpu.VMEM((lags, recv, wide), bf16),
            pltpu.VMEM((n_lag, depth, recv, wide), bf16),
            pltpu.VMEM((n_lag, 8, 128), jnp.int32),
            pltpu.VMEM((STEPS, scen, cols), f32),
            pltpu.VMEM((STEPS, scen, cols), jnp.int16),
            pltpu.VMEM((STEPS, scen, cols), jnp.int16),
            pltpu.VMEM((STEPS, CHUNKS, 8, 128), f32),
            pltpu.VMEM((STEPS, CHUNKS, 8, 128), f32),
            pltpu.VMEM((scen, cols), f32),
            pltpu.VMEM((n_lag, rows, cols), f32),
            pltpu.VMEM((rows, cols), f32),
            pltpu.VMEM((n_lag, rows, cols), bf16),
            pltpu.VMEM((rows, cols), bf16),
            pltpu.VMEM((n_lag, recv, wide), bf16),
            pltpu.VMEM((n_lag, recv, scen), f32),
            pltpu.VMEM((max(handlers, 1), recv, scen), f32),
            dma((depth,)), dma((depth, n_elem)), dma,
            dma((STEPS,)), dma((STEPS,)),
            dma((slots, nbits, n_elem)), dma((slots, nbits, n_elem)),
            dma((STEPS, CHUNKS)), dma((STEPS, CHUNKS)),
            dma((STEPS, CHUNKS)), dma((STEPS, CHUNKS)),
            dma((STEPS, CHUNKS)), dma((STEPS, CHUNKS)),
            dma((handlers,)), dma((n_lag,)),
            dma((handlers,)), dma((n_lag,)),
            dma((n_lag,)), dma,
            dma((n_lag,)), dma((n_lag,)),
            dma((n_lag,)), dma, dma, dma((n_lag,)),
            dma((n_lag,)), dma((n_lag,)),
        ],
        compiler_params=pltpu.CompilerParams(
            collective_id=0, has_side_effects=True, vmem_limit_bytes=60 * 1024 * 1024),
    )(kernel, past_rate, loading, initial_slip, peak_strength[None], cohesive_flags[None], patch_start[:, None],
      rad_kernel, bpad)
    return slip, traction, motion.T


def solution(mesh):
    n_lag, n_elem = mesh.shape["lag"], mesh.shape["elem"]
    return jax.shard_map(
        functools.partial(on_device, n_lag, n_elem, mesh.shape["scen"]),
        mesh=mesh,
        in_specs=(
            P("lag", "elem", None),
            P("lag", "scen", None),
            P("scen", "elem"),
            P("scen", "elem"),
            P("elem"),
            P("elem"),
            P("scen"),
            P(None, ("lag", "elem"), None),
            P(("lag", "elem"), None),
        ),
        out_specs=(
            P(("scen", "lag"), "elem"),
            P(("scen", "lag"), "elem"),
            P("scen", ("lag", "elem")),
        ),
        check_vma=False,
    )
```

```python
import functools

import jax
import jax.numpy as jnp
from jax import lax
from jax.experimental import pallas as pl
from jax.experimental.pallas import tpu as pltpu
from jax.sharding import PartitionSpec as P

STEPS = 4
SBLK = 16
PATCH = 128
OVERSTRESS = 2.0
WEAKEN = 0.5
CRITICAL = 0.5

CHUNKS = 4
LEVELS = 32767.0


def flip(e, bits):
    bit = 1
    while bit <= bits:
        if bits & bit:
            e = e + bit - 2 * bit * ((e // bit) % 2)
        bit *= 2
    return e


def nt(a, b):
    return lax.dot_general(a, b, (((1,), (1,)), ((), ())), preferred_element_type=jnp.float32)


def body(
    n_lag, n_elem, n_scen, near,
    kernel_h, past_h, loading, initial, peak, flags, patch, rad_h, bpad,
    slip_out, trac_out, motion_out,
    kern, hist, rad, radin, bin_v, psum, pout, pin, sout, sin, slip, trs, trin, rrs, rrin, rz, mpart, min_,
    ksem, psem, rsem,
    z_s, z_r, g_s, g_r, p_s, p_r, q_s, q_r, v_s, v_r, rad_s, rad_r, bm_s, bm_r, t_s, t_r, m_s, m_r, r_s, r_r, rz_s, rz_r, y_s, y_r,
):
    depth, cols, _ = kern.shape
    scen = psum.shape[1]
    NEW = STEPS - 1 + depth
    crow = scen // CHUNKS
    rows = scen // n_lag
    handlers = (rad_h.shape[0] - STEPS) // depth
    lag = lax.axis_index("lag")
    elem = lax.axis_index("elem")
    scn = lax.axis_index("scen")
    other = lax.rem(scn + 1, n_scen)
    half = depth // n_scen
    first = lag == 0
    later = lag > 0
    inner = lag < n_lag - 1
    up = lax.rem(lag + 1, n_lag)
    down = lax.rem(lag + n_lag - 1, n_lag)
    bits = []
    bit = n_elem // 2
    while bit:
        bits.append(bit)
        bit //= 2

    pending = []

    def remote(src, dst, ss, rs, **where):
        return pltpu.make_async_remote_copy(
            src_ref=src, dst_ref=dst, send_sem=ss, recv_sem=rs,
            device_id=where, device_id_type=pl.DeviceIdType.MESH)

    def go(desc, cond=None):
        if cond is None:
            desc.start()
        else:
            pl.when(cond)(desc.start)
        pending.append((cond, desc))

    kcopies = [pltpu.make_async_copy(kernel_h.at[i], kern.at[i], ksem.at[i]) for i in range(depth)]
    pcopies = [[pltpu.make_async_copy(past_h.at[i, :, pl.ds(q * cols, cols)], hist.at[STEPS - 1 + i, q], psem.at[i, q])
                for q in range(n_elem)] for i in range(depth)]
    rcopy = pltpu.make_async_copy(rad_h, rad, rsem)
    for i in range(depth):
        for c in pcopies[i]:
            c.start()
        kcopies[i].start()
    rcopy.start()

    barrier = pltpu.get_barrier_semaphore()

    def greet(k, c):
        pl.semaphore_signal(barrier, inc=1, device_id={"lag": lax.rem(lag + k, n_lag)},
                            device_id_type=pl.DeviceIdType.MESH)
        return c

    lax.fori_loop(1, n_lag, greet, 0)
    for b in bits:
        pl.semaphore_signal(barrier, inc=1, device_id={"elem": flip(elem, b)},
                            device_id_type=pl.DeviceIdType.MESH)
    pl.semaphore_signal(barrier, inc=1, device_id={"scen": other}, device_id_type=pl.DeviceIdType.MESH)
    pl.semaphore_wait(barrier, n_lag + len(bits))

    def stages():
        held = [0]
        out = []
        for b in bits:
            out.append((b, list(held)))
            held = held + [h ^ b for h in held]
        return out

    plan = stages()

    def g_desc(slot, k, n, off):
        b = plan[k][0]
        q = flip(elem, off)
        return remote(hist.at[slot, q], hist.at[slot, q], g_s.at[slot, k, n], g_r.at[slot, k, n],
                      elem=flip(elem, b))

    def g_start(slot, k, cond=None):
        for n, off in enumerate(plan[k][1]):
            go(g_desc(slot, k, n, off), cond)

    def g_wait(slot, k, cond=None):
        b = plan[k][0]

        def act():
            for n, off in enumerate(plan[k][1]):
                q = flip(flip(elem, off), b)
                remote(hist.at[slot, q], hist.at[slot, q], g_s.at[slot, k, n], g_r.at[slot, k, n],
                       elem=flip(elem, b)).wait_recv()
        act() if cond is None else pl.when(cond)(act)

    last = len(bits) - 1

    def g_rest(slot, cond=None):
        for k in range(len(bits)):
            g_wait(slot, k, cond)
            if k < last:
                g_start(slot, k + 1, cond)

    def z_desc(j):
        slot = STEPS - 2 - j
        return remote(past_h.at[depth - 1 - j, :, pl.ds(pl.multiple_of(elem * cols, cols), cols)],
                      hist.at[slot, elem], z_s.at[j], z_r.at[j], lag=up)

    for j in range(STEPS - 1):
        go(z_desc(j), inner)

    def mm(slot, i):
        acc = None
        for q in range(n_elem):
            term = nt(hist[slot, q], kern[i, :, q * cols:(q + 1) * cols])
            acc = term if acc is None else acc + term
        return acc

    lane = lax.broadcasted_iota(jnp.int32, (scen, cols), 1) + elem * cols
    begin = patch[...]
    weakening = WEAKEN * flags[...].astype(jnp.float32)

    @pl.when(first)
    def _():
        slip[...] = initial[...]

    def v_desc(t, c):
        part = hist.at[NEW + t, elem, pl.ds(c * crow, crow), :]
        return remote(part, part, v_s.at[t, c], v_r.at[t, c], lag=up)

    def relay_rate(t):
        for c in range(CHUNKS):
            pl.when(later)(v_desc(t, c).wait_recv)
            go(v_desc(t, c), inner & later)
        g_start(NEW + t, 0, later)

    for t in range(STEPS):
        acc = None
        for i in range(t, depth):
            if t == 0:
                for c in pcopies[i]:
                    c.wait()
                kcopies[i].wait()
            term = mm(STEPS - 1 + i - t, i)
            acc = term if acc is None else acc + term
        for i in range(1, t):
            acc = acc + mm(jnp.where(first, NEW + t - 1 - i, STEPS - 1 + i - t), i)
        psum[t] = acc
        if t:
            slot = STEPS - 1 - t
            g_rest(slot, later)
            g_rest(NEW + t - 1, first)
            psum[t] += mm(jnp.where(first, NEW + t - 1, slot), 0)
        if t < STEPS - 1:
            pl.when(later)(z_desc(t).wait_recv)
            g_start(STEPS - 2 - t, 0, later)
        for c in range(CHUNKS):
            span = pl.ds(c * crow, crow)

            def moves(c=c, span=span, t=t):
                return (remote(pout.at[t, span, :], pin.at[t, span, :], p_s.at[t, c], p_r.at[t, c], lag=down),
                        remote(sout.at[t, c], sin.at[t, c], q_s.at[t, c], q_r.at[t, c], lag=down))

            @pl.when(inner)
            def _(moves=moves, c=c, span=span, t=t):
                for move in moves():
                    move.wait_recv()
                psum[t, span, :] += pin[t, span, :].astype(jnp.int32).astype(jnp.float32) * sin[t, c, 0:1, 0:1]

            @pl.when(later)
            def _(c=c, span=span, t=t):
                value = psum[t, span, :]
                top = jnp.maximum(jnp.max(jnp.abs(value), axis=(0, 1), keepdims=True), 1e-30)
                pout[t, span, :] = jnp.floor(value * (LEVELS / top) + 0.5).astype(jnp.int32).astype(jnp.int16)
                sout[t, c] = jnp.broadcast_to(top / LEVELS, sout.shape[2:])
            for move in moves():
                go(move, later)

        @pl.when(first)
        def _(t=t):
            inside = jnp.where((lane >= begin) & (lane < begin + PATCH), 1.0, 0.0).astype(jnp.float32)
            traction = loading[...] + OVERSTRESS * inside + psum[t]
            now = slip[...]
            strength = peak[...] * (1.0 - weakening * now / (now + CRITICAL))
            rate = jnp.maximum(traction - strength, 0.0).astype(jnp.bfloat16)
            slip[...] = now + rate.astype(jnp.float32)
            hist[NEW + t, elem] = rate
            if t == STEPS - 1:
                for d in range(n_lag):
                    trs[d] = traction[d * rows:(d + 1) * rows]
                    rrs[d] = rate[d * rows:(d + 1) * rows]
        g_start(NEW + t, 0, first)
        if t < STEPS - 1:
            for c in range(CHUNKS):
                go(v_desc(t, c), first & inner)

        if t == STEPS - 1:
            go(remote(rad_h.at[0], rz.at[lag], rz_s, rz_r.at[lag], lag=0), later)
            for h in range(handlers):
                go(remote(bpad, bin_v.at[lag], bm_s.at[h], bm_r.at[lag], lag=h), lag != h)
                go(remote(rad_h.at[pl.ds(STEPS + h * depth + scn * half, half)],
                          radin.at[lag, pl.ds(scn * half, half)],
                          rad_s.at[h], rad_r.at[lag], lag=h), lag != h)
        if t >= 2:
            relay_rate(t - 2)
    for t in range(2, STEPS - 1):
        relay_rate(t)

    def t_desc(k):
        d = lax.rem(lag + k, n_lag)
        return remote(trs.at[d], trin, t_s.at[d], t_r, lag=d)

    def r_desc(k):
        d = lax.rem(lag + k, n_lag)
        return remote(rrs.at[d], rrin, r_s.at[d], r_r, lag=d)

    def y_desc(d, side):
        part = radin.at[d, pl.ds(side * half, half)]
        return remote(part, part, y_s.at[d], y_r.at[d], scen=other)

    def m_desc(d):
        return remote(mpart.at[d], min_.at[lag], m_s.at[d], m_r.at[lag], lag=d)

    @pl.when(first)
    def _():
        lax.fori_loop(1, n_lag, lambda k, c: (t_desc(k).start(), r_desc(k).start(), c)[2], 0)

    rcopy.wait()

    recv = motion_out.shape[0]
    width = kernel_h.shape[2] // SBLK
    per = cols // width

    def radiate(kernels, slots, blocks):
        masks = [[jnp.broadcast_to(blocks[0:1, k:k + 1], (recv, width)) == b for k in range(near)]
                 for b in range(SBLK)]
        acc = jnp.zeros((recv, scen), jnp.float32)
        for get, slot in zip(kernels, slots):
            value = get().astype(jnp.float32)
            for q in range(n_elem):
                spread = []
                for b in range(q * per, (q + 1) * per):
                    block = jnp.zeros((recv, width), jnp.float32)
                    for k in range(near):
                        block = jnp.where(masks[b][k], value[:, k * width:(k + 1) * width], block)
                    spread.append(block)
                acc = acc + nt(jnp.concatenate(spread, axis=1).astype(jnp.bfloat16), hist[slot, q])
        return acc

    @pl.when(lag < handlers)
    def _():
        def share(k, c):
            d = lax.rem(lag + k, n_lag)
            part = radin.at[d, pl.ds(scn * half, half)]
            remote(part, part, rad_s.at[0], rad_r.at[d], lag=0).wait_recv()
            y_desc(d, scn).start()
            return c
        lax.fori_loop(1, n_lag, share, 0)
        min_[lag] = radiate([lambda j=j: rad[STEPS + lag * depth + j] for j in range(depth)],
                            [STEPS - 1 + j for j in range(depth)], bpad[...])

        def one(k, c):
            d = lax.rem(lag + k, n_lag)
            y_desc(d, other).wait_recv()
            remote(bpad, bin_v.at[d], bm_s.at[0], bm_r.at[d], lag=0).wait_recv()
            mpart[d] = radiate([lambda j=j: radin[d, j] for j in range(depth)],
                               [STEPS - 1 + j for j in range(depth)], bin_v[d])
            pl.when(later)(m_desc(d).start)
            return c
        lax.fori_loop(1, n_lag, one, 0)

    g_rest(NEW + STEPS - 1, first)

    @pl.when(first)
    def _():
        def one(k, c):
            d = lax.rem(lag + k, n_lag)
            remote(rz.at[d], rz.at[d], rz_s, rz_r.at[d], lag=0).wait_recv()
            mpart[d] += radiate([lambda: rz[d]], [NEW + STEPS - 1], bin_v[d])
            m_desc(d).start()
            return c
        lax.fori_loop(1, n_lag, one, 0)
    for t in range(STEPS - 1):
        g_rest(NEW + t, later)
    motion_out[...] = radiate([lambda m=m: rad[m] for m in range(1, STEPS)],
                              [NEW + STEPS - 1 - m for m in range(1, STEPS)], bpad[...])

    @pl.when(first)
    def _():
        motion_out[...] += radiate([lambda: rad[0]], [NEW + STEPS - 1], bpad[...])

    @pl.when(first)
    def _():
        slip_out[...] = slip[0:rows]

    @pl.when(later)
    def _():
        remote(rrs.at[0], rrin, r_s.at[0], r_r, lag=0).wait_recv()
        whole = initial[...]
        for t in range(STEPS - 1):
            whole = whole + hist[NEW + t, elem].astype(jnp.float32)
        for d in range(1, n_lag):
            @pl.when(lag == d)
            def _(d=d):
                slip_out[...] = whole[d * rows:(d + 1) * rows] + rrin[...].astype(jnp.float32)

    @pl.when(first)
    def _():
        trac_out[...] = trs[0]

    @pl.when(later)
    def _():
        remote(trs.at[0], trin, t_s.at[0], t_r, lag=0).wait_recv()
        trac_out[...] = trin[...]

    for h in range(handlers):
        @pl.when(lag != h)
        def _(h=h):
            remote(mpart.at[0], min_.at[h], m_s.at[0], m_r.at[h], lag=h).wait_recv()
        motion_out[...] += min_[h]

    for cond, desc in pending:
        if cond is None:
            desc.wait_send()
        else:
            pl.when(cond)(desc.wait_send)

    @pl.when(first)
    def _():
        lax.fori_loop(1, n_lag, lambda k, c: (t_desc(k).wait_send(), r_desc(k).wait_send(), c)[2], 0)

    @pl.when(lag < handlers)
    def _():
        def one(k, c):
            d = lax.rem(lag + k, n_lag)
            y_desc(d, scn).wait_send()
            m_desc(d).wait_send()
            return c
        lax.fori_loop(1, n_lag, one, 0)


def on_device(n_lag, n_elem, n_scen, kernel, past_rate, loading, initial_slip, peak_strength, cohesive_flags, patch_start,
              rad_kernel, block_map):
    depth, cols, _ = kernel.shape
    scen = past_rate.shape[1]
    lags, recv, wide = rad_kernel.shape
    rows = scen // n_lag
    handlers = (lags - STEPS) // depth
    nbits = n_elem.bit_length() - 1
    bpad = jnp.pad(block_map, ((0, 7), (0, 128 - block_map.shape[1])))
    f32, bf16 = jnp.float32, jnp.bfloat16
    dma = pltpu.SemaphoreType.DMA
    vmem = pl.BlockSpec(memory_space=pltpu.VMEM)
    hbm = pl.BlockSpec(memory_space=pl.ANY)
    slots = 2 * STEPS - 1 + depth
    slip, traction, motion = pl.pallas_call(
        functools.partial(body, n_lag, n_elem, n_scen, block_map.shape[1]),
        out_shape=(
            jax.ShapeDtypeStruct((rows, cols), f32),
            jax.ShapeDtypeStruct((rows, cols), f32),
            jax.ShapeDtypeStruct((recv, scen), f32),
        ),
        in_specs=[hbm, hbm, vmem, vmem, vmem, vmem, vmem, hbm, vmem],
        out_specs=(vmem, vmem, vmem),
        scratch_shapes=[
            pltpu.VMEM((depth, cols, kernel.shape[2]), bf16),
            pltpu.VMEM((slots, n_elem, scen, cols), bf16),
            pltpu.VMEM((lags, recv, wide), bf16),
            pltpu.VMEM((n_lag, depth, recv, wide), bf16),
            pltpu.VMEM((n_lag, 8, 128), jnp.int32),
            pltpu.VMEM((STEPS, scen, cols), f32),
            pltpu.VMEM((STEPS, scen, cols), jnp.int16),
            pltpu.VMEM((STEPS, scen, cols), jnp.int16),
            pltpu.VMEM((STEPS, CHUNKS, 8, 128), f32),
            pltpu.VMEM((STEPS, CHUNKS, 8, 128), f32),
            pltpu.VMEM((scen, cols), f32),
            pltpu.VMEM((n_lag, rows, cols), f32),
            pltpu.VMEM((rows, cols), f32),
            pltpu.VMEM((n_lag, rows, cols), bf16),
            pltpu.VMEM((rows, cols), bf16),
            pltpu.VMEM((n_lag, recv, wide), bf16),
            pltpu.VMEM((n_lag, recv, scen), f32),
            pltpu.VMEM((max(handlers, 1), recv, scen), f32),
            dma((depth,)), dma((depth, n_elem)), dma,
            dma((STEPS,)), dma((STEPS,)),
            dma((slots, nbits, n_elem)), dma((slots, nbits, n_elem)),
            dma((STEPS, CHUNKS)), dma((STEPS, CHUNKS)),
            dma((STEPS, CHUNKS)), dma((STEPS, CHUNKS)),
            dma((STEPS, CHUNKS)), dma((STEPS, CHUNKS)),
            dma((handlers,)), dma((n_lag,)),
            dma((handlers,)), dma((n_lag,)),
            dma((n_lag,)), dma,
            dma((n_lag,)), dma((n_lag,)),
            dma((n_lag,)), dma, dma, dma((n_lag,)),
            dma((n_lag,)), dma((n_lag,)),
        ],
        compiler_params=pltpu.CompilerParams(
            collective_id=0, has_side_effects=True, vmem_limit_bytes=60 * 1024 * 1024),
    )(kernel, past_rate, loading, initial_slip, peak_strength[None], cohesive_flags[None], patch_start[:, None],
      rad_kernel, bpad)
    return slip, traction, motion.T


def solution(mesh):
    n_lag, n_elem = mesh.shape["lag"], mesh.shape["elem"]
    return jax.shard_map(
        functools.partial(on_device, n_lag, n_elem, mesh.shape["scen"]),
        mesh=mesh,
        in_specs=(
            P("lag", "elem", None),
            P("lag", "scen", None),
            P("scen", "elem"),
            P("scen", "elem"),
            P("elem"),
            P("elem"),
            P("scen"),
            P(None, ("lag", "elem"), None),
            P(("lag", "elem"), None),
        ),
        out_specs=(
            P(("scen", "lag"), "elem"),
            P(("scen", "lag"), "elem"),
            P("scen", ("lag", "elem")),
        ),
        check_vma=False,
    )
```
